32 devices in a mesh: shell: 4 (over y, x), band: 8 (over z, core).
Axes of the slice: x: 2, y: 2, z: 4, core: 2. Of those that a mesh axis runs over, the one named last changes fastest.
Arguments:
- density: float32 [8, 640, 1280], P('shell', 'band'), may hold values from -6 to 6
- momentum: float32 [8, 640, 1280], P('shell', 'band'), may hold values from -6 to 6
- observed: float32 [800, 2, 640], P('band'), may hold values from -12 to 12
- order_list: int32 [800], replicated, may hold values from 0 to 640, as said below
- shell_ratio: float32 [8], P('shell'), may hold values from 0.985 to 0.9995
- precision: float32 [640], replicated, may hold values from 0.03 to 0.3
Outputs:
- new_density: float32 [8, 640, 1280], P('shell', 'band')
- new_momentum: float32 [8, 640, 1280], P('shell', 'band')
The draws below stay inside these ranges and needn't reach their ends.
Inputs may be any that keep to these rules, and one draw needn't show every extreme that they name: `order_list`: each order 0 to 639 stands in exactly one slot; the value 640 marks an empty slot. The slots of band index d are entries d * 100 to (d + 1) * 100 - 1, live ones first; some band index has all 100 slots live.
All inputs are finite; a program needn't handle non-finite values.
Results may differ from the reference program's by a relative error of at most 0.0003.
Values sent between devices are 32-bit elements; how exact they have to be, the bound alone decides.
A program may use at most 192 MiB of HBM per device.

```python
import math
import jax
import jax.numpy as jnp
from jax import lax

DEG = 640
NLAT = 640
NLON = 1280
SHELLS = 8
SLOTS = 100
SLOTS_ALL = 800
N_BAND = 8


def draw_order_list(key, part):
    mean_count = DEG // N_BAND
    extra_count = SLOTS - mean_count
    place_key = jax.random.fold_in(key, 11)
    shift_key = jax.random.fold_in(key, 12)
    order_key = jax.random.fold_in(key, 13)
    shifts = jax.random.randint(shift_key, (N_BAND // 2,), 0, extra_count + 1)
    shifts = shifts.at[0].set(extra_count)
    signed = jnp.concatenate([shifts, -shifts])
    placed = jax.random.permutation(place_key, N_BAND)
    counts = mean_count + signed[placed]
    starts = jnp.cumsum(counts) - counts
    slot_index = jnp.arange(SLOTS)
    active = slot_index[None, :] < counts[:, None]
    chosen = jnp.minimum(starts[:, None] + slot_index[None, :], DEG - 1)
    shuffled = jax.random.permutation(order_key, DEG)
    return jnp.where(active, shuffled[chosen], DEG).reshape(-1).astype(jnp.int32)


def steps_of(stream_key, extent, pieces, least, high):
    level, own = 1.0, jax.random.fold_in(stream_key, 6)
    for axis_at, parts in pieces:
        heights = jnp.exp(jax.random.uniform(jax.random.fold_in(own, axis_at), (parts,), jnp.float32, least / len(pieces), high / len(pieces)))
        level = level * jnp.repeat(heights, extent[axis_at] // parts).reshape([-1 if axis == axis_at else 1 for axis in range(len(extent))])
    return level


def bell_draw(rng, dims, scale, reach, cuts=(), held_as=jnp.bfloat16):
    values = scale * jax.random.normal(rng, dims, jnp.float32)
    if cuts:
        values = values * steps_of(rng, dims, cuts, -0.22, 0.18)
    return jnp.clip(values, -reach, reach).astype(held_as)


def setup_inputs(seed: int = 0) -> dict:
    arg_keys = jax.random.split(jax.random.key(seed), 7)
    return {
        "density": bell_draw(arg_keys[0], (SHELLS, NLAT, NLON), 1.0, 6.0, ((0, 4), (1, 8)), jnp.float32),
        "momentum": bell_draw(arg_keys[1], (SHELLS, NLAT, NLON), 1.0, 6.0, ((0, 4), (1, 8)), jnp.float32),
        "observed": bell_draw(arg_keys[2], (SLOTS_ALL, 2, DEG), 2.0, 12.0, ((0, 8),), jnp.float32),
        "order_list": draw_order_list(jax.random.fold_in(arg_keys[6], 71), 0),
        "shell_ratio": jnp.clip(jnp.exp(math.log(0.9995) - 0.014613475 * jax.random.uniform(arg_keys[4], (SHELLS,), jnp.float32) ** steps_of(arg_keys[4], (SHELLS,), ((0, 4),), -0.2, 0.2)), 0.985, 0.9995),
        "precision": jnp.clip(jnp.exp(jax.random.uniform(arg_keys[5], (DEG,), jnp.float32, math.log(0.03), math.log(0.3))), 0.03, 0.3),
    }


STEP = 0.5
HIGH = lax.Precision.HIGHEST

def legendre_table(orders, lat_total, degrees):
    half_rows = lat_total // 2
    colatitude = (jnp.arange(half_rows, dtype=jnp.float32) + 0.5) * (jnp.pi / lat_total)
    cosine = jnp.cos(colatitude)[None, :]
    sine_row = jnp.sin(colatitude)[None, :]
    quadrature = jnp.sqrt(sine_row * (jnp.pi / lat_total))
    order_value = orders.astype(jnp.float32)[:, None]
    seed_log = order_value * jnp.log(sine_row) + 0.5 * (jnp.log(order_value + 0.5) + lax.lgamma(2.0 * order_value + 1.0) - order_value * jnp.log(4.0) - 2.0 * lax.lgamma(order_value + 1.0))
    number = orders.shape[0]
    span_rows = 64

    def one_span(position, carry):
        legendre, current, previous, scale_log = carry
        position = position.astype(jnp.int32)
        collected = []
        for offset_step in range(span_rows):
            offset = position * span_rows + offset_step
            inside = orders[:, None] + offset < degrees
            collected.append(jnp.where(inside, current * jnp.exp(scale_log) * quadrature, 0.0))
            next_step = (offset + 1).astype(jnp.float32)
            growth = jnp.sqrt((4.0 * (order_value + next_step) ** 2 - 1.0) / (next_step * (2.0 * order_value + next_step)))
            lower_sq = (order_value + next_step - 1.0) ** 2
            damping = jnp.sqrt((next_step - 1.0) * (2.0 * order_value + next_step - 1.0) / jnp.maximum(4.0 * lower_sq - 1.0, 1.0))
            current, previous = (growth * (cosine * current - damping * previous), current)
            if offset_step % 16 == 15:
                largest = jnp.maximum(jnp.abs(current), jnp.abs(previous))
                current = current / largest
                previous = previous / largest
                scale_log = scale_log + jnp.log(largest)
        rows_tile = jnp.stack(collected, axis=1).reshape(number, span_rows // 2, 2, half_rows)
        zero_index = jnp.zeros((), jnp.int32)
        legendre = lax.dynamic_update_slice(legendre, rows_tile, (zero_index, position * (span_rows // 2), zero_index, zero_index))
        return (legendre, current, previous, scale_log)
    initial = (jnp.zeros((number, degrees // 2, 2, half_rows), jnp.float32), jnp.ones((number, half_rows), jnp.float32), jnp.zeros((number, half_rows), jnp.float32), seed_log)
    return lax.fori_loop(0, degrees // span_rows, one_span, initial)[0]

def analyse(spectra, legendre):
    half_rows = spectra.shape[3] // 2
    northern = spectra[..., :half_rows]
    southern = jnp.flip(spectra[..., half_rows:], axis=3)
    folded = jnp.stack([northern + southern, northern - southern], axis=3)
    return jnp.einsum('bipz,bcspz->bcsip', legendre, folded, precision=HIGH, preferred_element_type=jnp.float32)

def synthesise(weighted, legendre):
    number, planes, shells, offsets = weighted.shape
    paired = weighted.reshape(number, planes, shells, offsets // 2, 2)
    folded = jnp.einsum('bipz,bcsip->bcspz', legendre, paired, precision=HIGH, preferred_element_type=jnp.float32)
    northern = folded[:, :, :, 0] + folded[:, :, :, 1]
    southern = jnp.flip(folded[:, :, :, 0] - folded[:, :, :, 1], axis=3)
    return jnp.concatenate([northern, southern], axis=3)

def likelihood(field_grid, observed, order_list, shell_ratio, precision):
    order_index = jnp.arange(DEG, dtype=jnp.int32)
    factor = jnp.where(order_index == 0, math.sqrt(1.0 / NLON), math.sqrt(2.0 / NLON)).astype(jnp.float32)
    spectra = jnp.fft.rfft(field_grid, axis=2)[:, :, :DEG]
    stacked = jnp.stack([jnp.real(spectra) * factor, jnp.imag(spectra) * factor])
    by_order = jnp.transpose(stacked, (3, 0, 1, 2))
    groups = jnp.arange(DEG, dtype=jnp.int32).reshape(DEG // 64, 64)

    def forward_group(group_item):
        return analyse(group_item[1], legendre_table(group_item[0], NLAT, DEG))
    shell_terms = lax.map(forward_group, (groups, by_order.reshape(DEG // 64, 64, 2, SHELLS, NLAT))).reshape(DEG, 2, SHELLS, DEG)
    degree_grid = (order_index[:, None] + order_index[None, :]).astype(jnp.float32)
    radial = jnp.exp(degree_grid[:, None, None, :] * jnp.log(shell_ratio)[None, None, :, None])
    summed = lax.optimization_barrier(jnp.sum(radial * shell_terms, axis=2))
    clipped = jnp.minimum(order_list, DEG - 1).astype(jnp.int32)
    padded = jnp.concatenate([precision, jnp.zeros_like(precision)])
    weights = jax.vmap(lambda first_degree: lax.dynamic_slice_in_dim(padded, first_degree, DEG))(order_list.astype(jnp.int32))[:, None, :]
    slot_residual = weights * (summed[clipped] - observed)
    residual = jnp.zeros((DEG, 2, DEG), jnp.float32).at[clipped].add(slot_residual)
    weighted = radial * residual[:, :, None, :]

    def adjoint_group(group_item):
        return synthesise(group_item[1], legendre_table(group_item[0], NLAT, DEG))
    adjoint = lax.map(adjoint_group, (groups, weighted.reshape(DEG // 64, 64, 2, SHELLS, DEG))).reshape(DEG, 2, SHELLS, NLAT)
    adjoint_t = jnp.transpose(adjoint, (1, 2, 3, 0))
    synth_scale = jnp.where(order_index == 0, NLON * math.sqrt(1.0 / NLON), 0.5 * NLON * math.sqrt(2.0 / NLON)).astype(jnp.float32)
    imag_keep = (order_index > 0).astype(jnp.float32)
    coefficients = adjoint_t[0] * synth_scale + 1j * (adjoint_t[1] * synth_scale * imag_keep)
    coefficients = jnp.pad(coefficients, ((0, 0), (0, 0), (0, NLON // 2 + 1 - DEG)))
    return jnp.fft.irfft(coefficients, n=NLON, axis=2)

def reference(density, momentum, observed, order_list, shell_ratio, precision):
    first_grad = likelihood(density, observed, order_list, shell_ratio, precision)
    half_momentum = momentum - 0.5 * STEP * (density + first_grad)
    new_density = density + STEP * half_momentum
    second_grad = likelihood(new_density, observed, order_list, shell_ratio, precision)
    new_momentum = half_momentum - 0.5 * STEP * (new_density + second_grad)
    return (new_density, new_momentum)
```

```python
import functools
import math

import jax
import jax.numpy as jnp
from jax import lax
from jax.experimental import pallas as pl
from jax.experimental.pallas import tpu as pltpu
from jax.sharding import PartitionSpec as P

STEP = 0.5
HIGH = lax.Precision.HIGH
SPAN = 64
RENORM = 16


def dot_ab(a, b):
    return lax.dot_general(a, b, (((1,), (0,)), ((), ())), preferred_element_type=jnp.float32)


def dot_abt(a, b):
    return lax.dot_general(a, b, (((1,), (1,)), ((), ())), preferred_element_type=jnp.float32)


def split_parts(x):
    top = x.astype(jnp.bfloat16)
    return top, (x - top.astype(jnp.float32)).astype(jnp.bfloat16)


def legendre_kernel(
    slots, grow_ref, damp_ref, first_ref, seed_ref, cos_ref, quad_ref, top_ref, low_ref,
    current_ref, previous_ref, log_ref, *lane_blocks,
):
    rows = current_ref.shape[0]
    half_rows = top_ref.shape[3]

    @pl.when(pl.program_id(0) == 0)
    def _():
        current_ref[...] = first_ref[...]
        previous_ref[...] = jnp.zeros_like(previous_ref)
        log_ref[...] = seed_ref[...]

    cosine = cos_ref[...]
    quadrature = quad_ref[...]

    for step in range(SPAN):
        if step % RENORM == 0:
            factor = jnp.exp(log_ref[...]) * quadrature
        current = current_ref[...]
        previous = previous_ref[...]
        value = current * factor
        for at, block in enumerate(lane_blocks):
            block[pl.ds(step * rows, rows), :] = value[:, at * 128 : (at + 1) * 128]
        growth = grow_ref[0, :, step : step + 1]
        damping = damp_ref[0, :, step : step + 1]
        following = growth * (cosine * current - damping * previous)
        if step % RENORM == RENORM - 1:
            largest = jnp.maximum(jnp.abs(following), jnp.abs(current))
            largest = jnp.where(largest == 0.0, 1.0, largest)
            current_ref[...] = following / largest
            previous_ref[...] = current / largest
            log_ref[...] = log_ref[...] + jnp.log(largest)
        else:
            current_ref[...] = following
            previous_ref[...] = current

    for slot in range(slots):
        for parity in range(2):
            for at, block in enumerate(lane_blocks):
                wide = min(128, half_rows - at * 128)
                values = block[pl.ds(parity * rows + slot, SPAN // 2, stride=2 * rows), :]
                top, low = split_parts(values)
                top_ref[slot, parity, :, at * 128 : at * 128 + wide] = top[:, :wide]
                low_ref[slot, parity, :, at * 128 : at * 128 + wide] = low[:, :wide]


def legendre_tables(orders, lat_total, degrees):
    slots = orders.shape[0]
    rows = -(-slots // 8) * 8
    half_rows = lat_total // 2
    padded = jnp.concatenate([orders, jnp.full((rows - slots,), degrees, orders.dtype)])
    lanes = -(-half_rows // 128) * 128
    row_at = jnp.minimum(jnp.arange(lanes), half_rows - 1)
    colatitude = (row_at.astype(jnp.float32) + 0.5) * (jnp.pi / lat_total)
    cosine = jnp.cos(colatitude)[None, :]
    sine_row = jnp.sin(colatitude)[None, :]
    quadrature = jnp.sqrt(sine_row * (jnp.pi / lat_total))
    order_value = padded.astype(jnp.float32)[:, None]
    seed_log = order_value * jnp.log(sine_row) + 0.5 * (
        jnp.log(order_value + 0.5)
        + lax.lgamma(2.0 * order_value + 1.0)
        - order_value * jnp.log(4.0)
        - 2.0 * lax.lgamma(order_value + 1.0)
    )
    next_int = jnp.arange(1, degrees + 1, dtype=jnp.int32)[None, :]
    next_step = next_int.astype(jnp.float32)
    growth = jnp.sqrt(
        (4.0 * (order_value + next_step) ** 2 - 1.0) / (next_step * (2.0 * order_value + next_step))
    )
    growth = jnp.where(padded[:, None] + next_int < degrees, growth, 0.0)
    lower_sq = (order_value + next_step - 1.0) ** 2
    damping = jnp.sqrt(
        (next_step - 1.0)
        * (2.0 * order_value + next_step - 1.0)
        / jnp.maximum(4.0 * lower_sq - 1.0, 1.0)
    )
    spans = degrees // SPAN
    growth = growth.reshape(rows, spans, SPAN).transpose(1, 0, 2)
    damping = damping.reshape(rows, spans, SPAN).transpose(1, 0, 2)
    first = jnp.broadcast_to(
        jnp.where(padded[:, None] < degrees, 1.0, 0.0).astype(jnp.float32), (rows, lanes)
    )
    whole = lambda shape: pl.BlockSpec(shape, lambda i: (0,) * len(shape))
    coefficient = pl.BlockSpec((1, rows, SPAN), lambda i: (i, 0, 0))
    out_block = pl.BlockSpec((slots, 2, SPAN // 2, half_rows), lambda i: (0, 0, i, 0))
    out_shape = jax.ShapeDtypeStruct((slots, 2, degrees // 2, half_rows), jnp.bfloat16)
    state = pltpu.VMEM((rows, lanes), jnp.float32)
    blocks = [pltpu.VMEM((SPAN * rows, 128), jnp.float32)] * (lanes // 128)
    return pl.pallas_call(
        functools.partial(legendre_kernel, slots),
        grid=(spans,),
        in_specs=[coefficient, coefficient, whole((rows, lanes)), whole((rows, lanes)),
                  whole((1, lanes)), whole((1, lanes))],
        out_specs=[out_block, out_block],
        out_shape=[out_shape, out_shape],
        scratch_shapes=[state, state, state] + blocks,
        name="legendre",
    )(growth, damping, first, seed_log, cosine, quadrature)


def flip_lanes(x, mirror):
    rows = x.shape[0]
    both = dot_ab(jnp.concatenate(split_parts(x), axis=0), mirror)
    return both[:rows] + both[rows:]


def misfit_kernel(
    shells, order_ref, field_ref, top_ref, low_ref, observed_ref, weight_ref, ratio_ref, mirror_ref,
    out_ref,
):
    rows = 2 * shells
    half = top_ref.shape[2]
    mirror = mirror_ref[...]
    order = order_ref[pl.program_id(0)]
    northern = field_ref[0, 0]
    southern = flip_lanes(field_ref[0, 1], mirror)
    log_ratio = ratio_ref[:, 0:1]
    pair = lax.broadcasted_iota(jnp.int32, (rows, half), 1)
    grids = []
    for parity in range(2):
        folded = northern + southern if parity == 0 else northern - southern
        top, low = split_parts(folded)
        main = dot_abt(jnp.concatenate([top, low], axis=0), top_ref[0, parity])
        terms = main[:rows] + main[rows:] + dot_abt(top, low_ref[0, parity])
        degree = (order + 2 * pair + parity).astype(jnp.float32)
        radial = jnp.exp(degree * log_ratio)
        terms = terms * radial
        weight = weight_ref[0, parity : parity + 1, :]
        pieces = []
        for part in range(2):
            total = jnp.sum(terms[part * shells : (part + 1) * shells], axis=0, keepdims=True)
            seen = observed_ref[0, 2 * parity + part : 2 * parity + part + 1, :]
            pieces.append(jnp.broadcast_to(weight * (total - seen), (shells, half)))
        weighted = radial * jnp.concatenate(pieces, axis=0)
        top, low = split_parts(weighted)
        main = dot_ab(jnp.concatenate([top, low], axis=0), top_ref[0, parity])
        grids.append(main[:rows] + main[rows:] + dot_ab(top, low_ref[0, parity]))
    out_ref[0, 0] = grids[0] + grids[1]
    out_ref[0, 1] = flip_lanes(grids[0] - grids[1], mirror)


def misfit(field, orders, tables, observed, weights, log_ratio, mirror):
    slots, _, rows, half_rows = field.shape
    half = tables[0].shape[2]
    at_slot = lambda shape: pl.BlockSpec((1,) + shape, lambda i, o: (i,) + (0,) * len(shape))
    whole = lambda shape: pl.BlockSpec(shape, lambda i, o: (0,) * len(shape))
    return pl.pallas_call(
        functools.partial(misfit_kernel, rows // 2),
        grid_spec=pltpu.PrefetchScalarGridSpec(
            num_scalar_prefetch=1,
            grid=(slots,),
            in_specs=[at_slot((2, rows, half_rows)), at_slot((2, half, half_rows)),
                      at_slot((2, half, half_rows)), at_slot((4, half)), at_slot((2, half)),
                      whole(log_ratio.shape), whole(mirror.shape)],
            out_specs=at_slot((2, rows, half_rows)),
        ),
        out_shape=jax.ShapeDtypeStruct(field.shape, jnp.float32),
        name="misfit",
    )(orders, field, tables[0], tables[1], observed, weights, log_ratio, mirror)


def fourier_tables(orders, lon_cells):
    block = math.gcd(lon_cells, 128)
    blocks = lon_cells // block
    scale = 2.0 * jnp.pi / lon_cells
    coarse = (orders[:, None] * (block * jnp.arange(blocks, dtype=jnp.int32))[None, :]) % lon_cells
    fine = (orders[:, None] * jnp.arange(block, dtype=jnp.int32)[None, :]) % lon_cells
    coarse = coarse.astype(jnp.float32) * scale
    fine = fine.astype(jnp.float32) * scale
    factor = jnp.where(
        orders == 0, math.sqrt(1.0 / lon_cells), math.sqrt(2.0 / lon_cells)
    ).astype(jnp.float32)[:, None]
    coarse_cos, coarse_sin = factor * jnp.cos(coarse), factor * jnp.sin(coarse)
    fine_cos, fine_sin = jnp.cos(fine), jnp.sin(fine)
    cos_parts, sin_parts = [], []
    for at in range(blocks):
        c, s = coarse_cos[:, at : at + 1], coarse_sin[:, at : at + 1]
        cos_parts.append(c * fine_cos - s * fine_sin)
        sin_parts.append(-(s * fine_cos + c * fine_sin))
    return jnp.concatenate(cos_parts, axis=1), jnp.concatenate(sin_parts, axis=1)


def degree_weights(precision, orders, degrees):
    values = jnp.broadcast_to(
        jnp.concatenate([precision, jnp.zeros_like(precision)])[None, :],
        (orders.shape[0], 2 * degrees),
    )
    bit = 1
    while bit <= degrees:
        moved = jnp.concatenate([values[:, bit:], jnp.zeros_like(values[:, :bit])], axis=1)
        values = jnp.where((orders[:, None] & bit) != 0, moved, values)
        bit *= 2
    return values[:, :degrees]


def body(density, momentum, observed, order_list, shell_ratio, precision):
    degrees = observed.shape[2]
    local_shells, lat_rows, lon_cells = density.shape
    n_shell, n_band = lax.axis_size("shell"), lax.axis_size("band")
    lat_total, shells = lat_rows * n_band, local_shells * n_shell
    devices = n_shell * n_band
    own = observed.shape[0] // n_shell
    half, half_rows = degrees // 2, lat_total // 2
    cells = local_shells * lat_rows

    by_device = order_list.reshape(n_band, n_shell, own).transpose(1, 0, 2).reshape(-1)
    cos_table, sin_table = fourier_tables(by_device, lon_cells)
    start = lax.axis_index("shell") * own
    own_orders = lax.dynamic_slice_in_dim(
        order_list, lax.axis_index("band") * observed.shape[0] + start, own
    )
    own_observed = lax.dynamic_slice_in_dim(observed, start, own)
    own_observed = own_observed.reshape(own, 2, half, 2).transpose(0, 3, 1, 2).reshape(own, 4, half)
    weights = degree_weights(precision, own_orders, degrees)
    weights = weights.reshape(own, half, 2).transpose(0, 2, 1)
    tables = legendre_tables(own_orders, lat_total, degrees)
    row_at = jnp.arange(half_rows)
    mirror = (row_at[:, None] + row_at[None, :] == half_rows - 1).astype(jnp.bfloat16)
    own_ratio = jnp.broadcast_to(jnp.log(shell_ratio)[None, None, :], (devices, own, local_shells))

    def exchange(x):
        return lax.all_to_all(x, ("shell", "band"), split_axis=0, concat_axis=0, tiled=True)

    def likelihood_grid(field_grid, log_ratio):
        flat = field_grid.reshape(cells, lon_cells)
        sent = jnp.concatenate(
            [
                jnp.einsum("tn,rn->tr", table, flat, precision=HIGH,
                           preferred_element_type=jnp.float32)
                for table in (cos_table, sin_table)
            ],
            axis=1,
        ).reshape(devices, own, 2 * cells)
        if log_ratio is None:
            received = exchange(jnp.concatenate([sent, own_ratio], axis=2))
            log_ratio = received[:, 0, 2 * cells :].reshape(n_shell, n_band, local_shells)[:, 0]
            log_ratio = jnp.tile(log_ratio.reshape(shells), 2)[:, None]
            log_ratio = jnp.broadcast_to(log_ratio, (2 * shells, 128))
            received = received[:, :, : 2 * cells]
        else:
            received = exchange(sent)
        split = received.reshape(n_shell, 2, n_band // 2, own, 2, local_shells, lat_rows)
        field = split.transpose(3, 1, 4, 0, 5, 2, 6).reshape(own, 2, 2 * shells, half_rows)
        result = misfit(field, own_orders, tables, own_observed, weights, log_ratio, mirror)
        result = result.reshape(own, 2, 2, n_shell, local_shells, n_band // 2, lat_rows)
        result = result.transpose(3, 1, 5, 0, 2, 4, 6).reshape(devices, own, 2 * cells)
        returned = exchange(result).reshape(devices * own, 2 * cells)
        grid = jnp.einsum(
            "tr,tn->rn", returned[:, :cells], cos_table, precision=HIGH,
            preferred_element_type=jnp.float32,
        ) + jnp.einsum(
            "tr,tn->rn", returned[:, cells:], sin_table, precision=HIGH,
            preferred_element_type=jnp.float32,
        )
        return grid.reshape(field_grid.shape), log_ratio

    first_grad, log_ratio = likelihood_grid(density, None)
    half_momentum = momentum - 0.5 * STEP * (density + first_grad)
    new_density = density + STEP * half_momentum
    second_grad, _ = likelihood_grid(new_density, log_ratio)
    new_momentum = half_momentum - 0.5 * STEP * (new_density + second_grad)
    return (new_density, new_momentum)


def solution(mesh):
    in_specs = (
        P("shell", "band", None),
        P("shell", "band", None),
        P("band", None, None),
        P(),
        P("shell"),
        P(),
    )
    out_specs = (P("shell", "band", None), P("shell", "band", None))
    return jax.shard_map(body, mesh=mesh, in_specs=in_specs, out_specs=out_specs, check_vma=False)
```

```python
import functools
import math

import jax
import jax.numpy as jnp
from jax import lax
from jax.experimental import pallas as pl
from jax.experimental.pallas import tpu as pltpu
from jax.sharding import PartitionSpec as P

STEP = 0.5
HIGH = lax.Precision.HIGH
SPAN = 64
RENORM = 16


def dot_ab(a, b):
    return lax.dot_general(a, b, (((1,), (0,)), ((), ())), preferred_element_type=jnp.float32)


def dot_abt(a, b):
    return lax.dot_general(a, b, (((1,), (1,)), ((), ())), preferred_element_type=jnp.float32)


def split_parts(x):
    top = x.astype(jnp.bfloat16)
    return top, (x - top.astype(jnp.float32)).astype(jnp.bfloat16)


def legendre_kernel(
    slots, grow_ref, damp_ref, first_ref, seed_ref, cos_ref, quad_ref, top_ref, low_ref,
    current_ref, previous_ref, log_ref, *lane_blocks,
):
    rows = current_ref.shape[0]
    half_rows = top_ref.shape[3]

    @pl.when(pl.program_id(0) == 0)
    def _():
        current_ref[...] = first_ref[...]
        previous_ref[...] = jnp.zeros_like(previous_ref)
        log_ref[...] = seed_ref[...]

    cosine = cos_ref[...]
    quadrature = quad_ref[...]

    for step in range(SPAN):
        if step % RENORM == 0:
            factor = jnp.exp(log_ref[...]) * quadrature
        current = current_ref[...]
        previous = previous_ref[...]
        value = current * factor
        for at, block in enumerate(lane_blocks):
            block[pl.ds(step * rows, rows), :] = value[:, at * 128 : (at + 1) * 128]
        growth = grow_ref[0, :, step : step + 1]
        damping = damp_ref[0, :, step : step + 1]
        following = growth * (cosine * current - damping * previous)
        if step % RENORM == RENORM - 1:
            largest = jnp.maximum(jnp.abs(following), jnp.abs(current))
            largest = jnp.where(largest == 0.0, 1.0, largest)
            current_ref[...] = following / largest
            previous_ref[...] = current / largest
            log_ref[...] = log_ref[...] + jnp.log(largest)
        else:
            current_ref[...] = following
            previous_ref[...] = current

    for slot in range(slots):
        for parity in range(2):
            for at, block in enumerate(lane_blocks):
                wide = min(128, half_rows - at * 128)
                values = block[pl.ds(parity * rows + slot, SPAN // 2, stride=2 * rows), :]
                top, low = split_parts(values)
                top_ref[slot, parity, :, at * 128 : at * 128 + wide] = top[:, :wide]
                low_ref[slot, parity, :, at * 128 : at * 128 + wide] = low[:, :wide]


def legendre_tables(orders, lat_total, degrees):
    slots = orders.shape[0]
    rows = -(-slots // 8) * 8
    half_rows = lat_total // 2
    padded = jnp.concatenate([orders, jnp.full((rows - slots,), degrees, orders.dtype)])
    lanes = -(-half_rows // 128) * 128
    row_at = jnp.minimum(jnp.arange(lanes), half_rows - 1)
    colatitude = (row_at.astype(jnp.float32) + 0.5) * (jnp.pi / lat_total)
    cosine = jnp.cos(colatitude)[None, :]
    sine_row = jnp.sin(colatitude)[None, :]
    quadrature = jnp.sqrt(sine_row * (jnp.pi / lat_total))
    order_value = padded.astype(jnp.float32)[:, None]
    seed_log = order_value * jnp.log(sine_row) + 0.5 * (
        jnp.log(order_value + 0.5)
        + lax.lgamma(2.0 * order_value + 1.0)
        - order_value * jnp.log(4.0)
        - 2.0 * lax.lgamma(order_value + 1.0)
    )
    next_int = jnp.arange(1, degrees + 1, dtype=jnp.int32)[None, :]
    next_step = next_int.astype(jnp.float32)
    growth = jnp.sqrt(
        (4.0 * (order_value + next_step) ** 2 - 1.0) / (next_step * (2.0 * order_value + next_step))
    )
    growth = jnp.where(padded[:, None] + next_int < degrees, growth, 0.0)
    lower_sq = (order_value + next_step - 1.0) ** 2
    damping = jnp.sqrt(
        (next_step - 1.0)
        * (2.0 * order_value + next_step - 1.0)
        / jnp.maximum(4.0 * lower_sq - 1.0, 1.0)
    )
    spans = degrees // SPAN
    growth = growth.reshape(rows, spans, SPAN).transpose(1, 0, 2)
    damping = damping.reshape(rows, spans, SPAN).transpose(1, 0, 2)
    first = jnp.broadcast_to(
        jnp.where(padded[:, None] < degrees, 1.0, 0.0).astype(jnp.float32), (rows, lanes)
    )
    whole = lambda shape: pl.BlockSpec(shape, lambda i: (0,) * len(shape))
    coefficient = pl.BlockSpec((1, rows, SPAN), lambda i: (i, 0, 0))
    out_block = pl.BlockSpec((slots, 2, SPAN // 2, half_rows), lambda i: (0, 0, i, 0))
    out_shape = jax.ShapeDtypeStruct((slots, 2, degrees // 2, half_rows), jnp.bfloat16)
    state = pltpu.VMEM((rows, lanes), jnp.float32)
    blocks = [pltpu.VMEM((SPAN * rows, 128), jnp.float32)] * (lanes // 128)
    return pl.pallas_call(
        functools.partial(legendre_kernel, slots),
        grid=(spans,),
        in_specs=[coefficient, coefficient, whole((rows, lanes)), whole((rows, lanes)),
                  whole((1, lanes)), whole((1, lanes))],
        out_specs=[out_block, out_block],
        out_shape=[out_shape, out_shape],
        scratch_shapes=[state, state, state] + blocks,
        name="legendre",
    )(growth, damping, first, seed_log, cosine, quadrature)


def flip_lanes(x, mirror):
    rows = x.shape[0]
    both = dot_ab(jnp.concatenate(split_parts(x), axis=0), mirror)
    return both[:rows] + both[rows:]


def misfit_kernel(
    shells, order_ref, field_ref, top_ref, low_ref, observed_ref, weight_ref, ratio_ref, mirror_ref,
    out_ref,
):
    rows = 2 * shells
    half = top_ref.shape[2]
    mirror = mirror_ref[...]
    order = order_ref[pl.program_id(0)]
    northern = field_ref[0, 0]
    southern = flip_lanes(field_ref[0, 1], mirror)
    log_ratio = ratio_ref[:, 0:1]
    precision = weight_ref[...]
    wide = precision.shape[1]
    pair = lax.broadcasted_iota(jnp.int32, (rows, half), 1)
    grids = []
    for parity in range(2):
        folded = northern + southern if parity == 0 else northern - southern
        top, low = split_parts(folded)
        main = dot_abt(jnp.concatenate([top, low], axis=0), top_ref[0, parity])
        terms = main[:rows] + main[rows:] + dot_abt(top, low_ref[0, parity])
        degree = (order + 2 * pair + parity).astype(jnp.float32)
        radial = jnp.exp(degree * log_ratio)
        terms = terms * radial
        first = order + parity
        moved = pltpu.roll(precision, lax.rem(wide - first // 2, wide), 1)[:, :half]
        weight = jnp.where(first % 2 == 0, moved[0:1], moved[1:2])
        pieces = []
        for part in range(2):
            total = jnp.sum(terms[part * shells : (part + 1) * shells], axis=0, keepdims=True)
            seen = observed_ref[0, 2 * parity + part : 2 * parity + part + 1, :]
            pieces.append(jnp.broadcast_to(weight * (total - seen), (shells, half)))
        weighted = radial * jnp.concatenate(pieces, axis=0)
        top, low = split_parts(weighted)
        main = dot_ab(jnp.concatenate([top, low], axis=0), top_ref[0, parity])
        grids.append(main[:rows] + main[rows:] + dot_ab(top, low_ref[0, parity]))
    out_ref[0, 0] = grids[0] + grids[1]
    out_ref[0, 1] = flip_lanes(grids[0] - grids[1], mirror)


def misfit(field, orders, tables, observed, weights, log_ratio, mirror):
    slots, _, rows, half_rows = field.shape
    half = tables[0].shape[2]
    at_slot = lambda shape: pl.BlockSpec((1,) + shape, lambda i, o: (i,) + (0,) * len(shape))
    whole = lambda shape: pl.BlockSpec(shape, lambda i, o: (0,) * len(shape))
    return pl.pallas_call(
        functools.partial(misfit_kernel, rows // 2),
        grid_spec=pltpu.PrefetchScalarGridSpec(
            num_scalar_prefetch=1,
            grid=(slots,),
            in_specs=[at_slot((2, rows, half_rows)), at_slot((2, half, half_rows)),
                      at_slot((2, half, half_rows)), at_slot((4, half)), whole(weights.shape),
                      whole(log_ratio.shape), whole(mirror.shape)],
            out_specs=at_slot((2, rows, half_rows)),
        ),
        out_shape=jax.ShapeDtypeStruct(field.shape, jnp.float32),
        name="misfit",
    )(orders, field, tables[0], tables[1], observed, weights, log_ratio, mirror)


def fourier_kernel(coarse_cos, coarse_sin, fine_cos, fine_sin, cos_ref, sin_ref):
    block = fine_cos.shape[1]
    fine_c, fine_s = fine_cos[...], fine_sin[...]
    for at in range(coarse_cos.shape[1]):
        c, s = coarse_cos[:, at : at + 1], coarse_sin[:, at : at + 1]
        cos_ref[:, at * block : (at + 1) * block] = c * fine_c - s * fine_s
        sin_ref[:, at * block : (at + 1) * block] = -(s * fine_c + c * fine_s)


def fourier_tables(orders, lon_cells):
    block = math.gcd(lon_cells, 128)
    blocks = lon_cells // block
    scale = 2.0 * jnp.pi / lon_cells
    coarse = (orders[:, None] * (block * jnp.arange(blocks, dtype=jnp.int32))[None, :]) % lon_cells
    fine = (orders[:, None] * jnp.arange(block, dtype=jnp.int32)[None, :]) % lon_cells
    coarse = coarse.astype(jnp.float32) * scale
    fine = fine.astype(jnp.float32) * scale
    factor = jnp.where(
        orders == 0, math.sqrt(1.0 / lon_cells), math.sqrt(2.0 / lon_cells)
    ).astype(jnp.float32)[:, None]
    coarse_cos, coarse_sin = factor * jnp.cos(coarse), factor * jnp.sin(coarse)
    fine_cos, fine_sin = jnp.cos(fine), jnp.sin(fine)
    rows = orders.shape[0]
    tall = max(d for d in range(8, 201, 8) if rows % d == 0)
    at_rows = lambda width: pl.BlockSpec((tall, width), lambda i: (i, 0))
    table = jax.ShapeDtypeStruct((rows, lon_cells), jnp.float32)
    return pl.pallas_call(
        fourier_kernel,
        grid=(rows // tall,),
        in_specs=[at_rows(blocks), at_rows(blocks), at_rows(block), at_rows(block)],
        out_specs=[at_rows(lon_cells), at_rows(lon_cells)],
        out_shape=[table, table],
        name="fourier",
    )(coarse_cos, coarse_sin, fine_cos, fine_sin)


def body(density, momentum, observed, order_list, shell_ratio, precision):
    degrees = observed.shape[2]
    local_shells, lat_rows, lon_cells = density.shape
    n_shell, n_band = lax.axis_size("shell"), lax.axis_size("band")
    lat_total, shells = lat_rows * n_band, local_shells * n_shell
    devices = n_shell * n_band
    own = observed.shape[0] // n_shell
    half, half_rows = degrees // 2, lat_total // 2
    cells = local_shells * lat_rows

    by_device = order_list.reshape(n_band, n_shell, own).transpose(1, 0, 2).reshape(-1)
    cos_table, sin_table = fourier_tables(by_device, lon_cells)
    start = lax.axis_index("shell") * own
    own_orders = lax.dynamic_slice_in_dim(
        order_list, lax.axis_index("band") * observed.shape[0] + start, own
    )
    own_observed = lax.dynamic_slice_in_dim(observed, start, own)
    own_observed = own_observed.reshape(own, 2, half, 2).transpose(0, 3, 1, 2).reshape(own, 4, half)
    weights = jnp.zeros((8, -(-(degrees + 1) // 128) * 128), jnp.float32)
    weights = lax.dynamic_update_slice(weights, precision.reshape(half, 2).T, (0, 0))
    tables = legendre_tables(own_orders, lat_total, degrees)
    row_at = jnp.arange(half_rows)
    mirror = (row_at[:, None] + row_at[None, :] == half_rows - 1).astype(jnp.bfloat16)
    own_ratio = jnp.broadcast_to(jnp.log(shell_ratio)[None, None, :], (devices, own, local_shells))

    def exchange(x):
        return lax.all_to_all(x, ("shell", "band"), split_axis=0, concat_axis=0, tiled=True)

    def likelihood_grid(field_grid, log_ratio):
        flat = field_grid.reshape(cells, lon_cells)
        sent = jnp.concatenate(
            [
                jnp.einsum("tn,rn->tr", table, flat, precision=HIGH,
                           preferred_element_type=jnp.float32)
                for table in (cos_table, sin_table)
            ],
            axis=1,
        ).reshape(devices, own, 2 * cells)
        if log_ratio is None:
            received = exchange(jnp.concatenate([sent, own_ratio], axis=2))
            log_ratio = received[:, 0, 2 * cells :].reshape(n_shell, n_band, local_shells)[:, 0]
            log_ratio = jnp.tile(log_ratio.reshape(shells), 2)[:, None]
            log_ratio = jnp.broadcast_to(log_ratio, (2 * shells, 128))
            received = received[:, :, : 2 * cells]
        else:
            received = exchange(sent)
        split = received.reshape(n_shell, 2, n_band // 2, own, 2, local_shells, lat_rows)
        field = split.transpose(3, 1, 4, 0, 5, 2, 6).reshape(own, 2, 2 * shells, half_rows)
        result = misfit(field, own_orders, tables, own_observed, weights, log_ratio, mirror)
        result = result.reshape(own, 2, 2, n_shell, local_shells, n_band // 2, lat_rows)
        result = result.transpose(3, 1, 5, 0, 2, 4, 6).reshape(devices, own, 2 * cells)
        returned = exchange(result).reshape(devices * own, 2 * cells)
        grid = jnp.einsum(
            "tr,tn->rn", returned[:, :cells], cos_table, precision=HIGH,
            preferred_element_type=jnp.float32,
        ) + jnp.einsum(
            "tr,tn->rn", returned[:, cells:], sin_table, precision=HIGH,
            preferred_element_type=jnp.float32,
        )
        return grid.reshape(field_grid.shape), log_ratio

    first_grad, log_ratio = likelihood_grid(density, None)
    half_momentum = momentum - 0.5 * STEP * (density + first_grad)
    new_density = density + STEP * half_momentum
    second_grad, _ = likelihood_grid(new_density, log_ratio)
    new_momentum = half_momentum - 0.5 * STEP * (new_density + second_grad)
    return (new_density, new_momentum)


def solution(mesh):
    in_specs = (
        P("shell", "band", None),
        P("shell", "band", None),
        P("band", None, None),
        P(),
        P("shell"),
        P(),
    )
    out_specs = (P("shell", "band", None), P("shell", "band", None))
    return jax.shard_map(body, mesh=mesh, in_specs=in_specs, out_specs=out_specs, check_vma=False)
```
